256 devices in a mesh: tok: 16 (over y, x), ch: 16 (over z, core).
Axes of the slice: x: 4, y: 4, z: 8, core: 2. Of those that a mesh axis runs over, the one named last changes fastest.
Arguments:
- tokens: bfloat16 [256, 16384], P('tok', 'ch'), may hold values from -64 to 64
- probe: int32 [256, 16384], P('tok', 'ch'), may hold values from 0 to 1
- signs: int32 [16384], P('ch'), may hold values from 0 to 1
- gate_weight: bfloat16 [16384, 26624], P('ch', 'tok'), may hold values from -0.046875 to 0.046875
- up_weight: bfloat16 [16384, 26624], P('ch', 'tok'), may hold values from -0.046875 to 0.046875
- down_weight: bfloat16 [26624, 16384], P('tok', 'ch'), may hold values from -0.0390625 to 0.0390625
Outputs:
- rotated_product: float32 [256, 16384], P('tok', 'ch')
- diagonal_estimate: float32 [16384], P('ch')
The draws below stay inside these ranges and needn't reach their ends.
All inputs are finite; a program needn't handle non-finite values.
Results may differ from the reference program's by a relative error of at most 0.004.
Values may be sent and summed in bfloat16 or wider, within the bound.
No kernel may reach another device: no remote copies, remote signals or barrier semaphores. Data moves between devices by JAX's collectives and lax.ppermute only.
A program may use at most 128 MiB of HBM per device.

```python
import math
import jax
import jax.numpy as jnp
from jax import lax

D = 16384
FF = 26624
TOKENS = 256


def draw_tokens(key, part):
    base_key, row_key, column_key = jax.random.split(key, 3)
    position = jnp.arange(TOKENS, dtype=jnp.float32) / max(TOKENS - 1, 1)
    row_factor = jnp.exp(jax.random.uniform(row_key, (TOKENS,), jnp.float32, math.log(0.6), math.log(1.5)))
    column_factor = jnp.exp(jax.random.uniform(column_key, (D,), jnp.float32, math.log(0.75), math.log(1.3)))
    values = jnp.clip(jax.random.normal(base_key, (TOKENS, D), jnp.float32), -6.0, 6.0)
    row_trend = jnp.exp(math.log(1.75) * position)
    return (values * (row_trend * row_factor)[:, None] * column_factor[None, :]).astype(jnp.bfloat16)


def touch_ends(drawn, stream_key, low, largest):
    dims = drawn.shape
    index_at = [jax.random.randint(jax.random.fold_in(stream_key, axis), (), 0, dims[axis]) for axis in range(len(dims))]
    drawn = drawn.at[tuple(index_at)].set(low)
    longest = dims.index(max(dims))
    index_at[longest] = (index_at[longest] + 1) % dims[longest]
    return drawn.at[tuple(index_at)].set(largest)


def level_of(stream_key, extent, pieces, smallest, top_value):
    def one(dim, parts):
        heights = jax.random.uniform(jax.random.fold_in(jax.random.fold_in(stream_key, 6), dim), (parts,), jnp.float32, smallest / len(pieces), top_value / len(pieces))
        return jnp.repeat(jnp.exp(heights), extent[dim] // parts).reshape((-1,) + (1,) * (len(extent) - dim - 1))

    factor_of = one(*pieces[0])
    for cut in pieces[1:]:
        factor_of = factor_of * one(*cut)
    return factor_of


def normal_values(rng, dims, spread, reach, cuts=(), kind=jnp.bfloat16):
    values = spread * jax.random.normal(rng, dims, jnp.float32)
    if cuts:
        values = values * level_of(rng, dims, cuts, -0.22, 0.18)
    return jnp.clip(values, -reach, reach).astype(kind)


def setup_inputs(seed: int = 0) -> dict:
    key_list = jax.random.split(jax.random.key(seed), 7)
    tokens = draw_tokens(jax.random.fold_in(key_list[6], 71), 0)
    probe = touch_ends(jax.random.randint(key_list[1], (TOKENS, D), 0, 2), jax.random.fold_in(key_list[1], 1), 0, 1).astype(jnp.int32)
    signs = touch_ends(jax.random.randint(key_list[2], (D,), 0, 2), jax.random.fold_in(key_list[2], 1), 0, 1).astype(jnp.int32)
    gate_weight = normal_values(key_list[3], (D, FF), D ** -0.5, 0.046875, ((0, 16), (1, 16)))
    up_weight = normal_values(key_list[4], (D, FF), D ** -0.5, 0.046875, ((0, 16), (1, 16)))
    down_weight = normal_values(key_list[5], (FF, D), FF ** -0.5, 0.0390625, ((0, 16), (1, 16)))
    return {"tokens": tokens, "probe": probe, "signs": signs, "gate_weight": gate_weight, "up_weight": up_weight, "down_weight": down_weight}


def walsh_transform(values):
    row_total, length = values.shape
    for bit_pos in range(length.bit_length() - 1):
        span_width = 2 ** bit_pos
        blocks = values.reshape(row_total, length // (2 * span_width), 2, span_width)
        lower_half = blocks[:, :, 0]
        upper_half = blocks[:, :, 1]
        values = jnp.stack([lower_half + upper_half, lower_half - upper_half], axis=2).reshape(row_total, length)
    return values

def reference(tokens, probe, signs, gate_weight, up_weight, down_weight):
    probe_signs = (2 * probe - 1).astype(jnp.float32)
    channel_signs = (2 * signs - 1).astype(jnp.float32)
    root_scale = 1.0 / math.sqrt(D)
    tangent = (walsh_transform(probe_signs * channel_signs[None, :]) * root_scale).astype(jnp.bfloat16)
    gate_pre = jnp.dot(tokens, gate_weight, preferred_element_type=jnp.float32)
    up_pre = jnp.dot(tokens, up_weight, preferred_element_type=jnp.float32)
    gate_tan = jnp.dot(tangent, gate_weight, preferred_element_type=jnp.float32)
    up_tan = jnp.dot(tangent, up_weight, preferred_element_type=jnp.float32)
    sigmoid_gate = jax.nn.sigmoid(gate_pre)
    activated = gate_pre * sigmoid_gate
    slope_term = sigmoid_gate * (1.0 + gate_pre * (1.0 - sigmoid_gate))
    hidden_tan = (slope_term * gate_tan * up_pre + activated * up_tan).astype(jnp.bfloat16)
    out_tangent = jnp.dot(hidden_tan, down_weight, preferred_element_type=jnp.float32).astype(jnp.bfloat16)
    back_hidden = jnp.dot(out_tangent, down_weight.T, preferred_element_type=jnp.float32)
    back_gate = (back_hidden * up_pre * slope_term).astype(jnp.bfloat16)
    back_up = (back_hidden * activated).astype(jnp.bfloat16)
    back_tokens = jnp.dot(back_gate, gate_weight.T, preferred_element_type=jnp.float32) + jnp.dot(back_up, up_weight.T, preferred_element_type=jnp.float32)
    rotated_product = walsh_transform(back_tokens) * root_scale * channel_signs[None, :]
    diagonal_estimate = lax.optimization_barrier(jnp.sum(probe_signs * rotated_product, axis=0)) / TOKENS
    return (rotated_product, diagonal_estimate)
```

```python
import math

import jax
import jax.numpy as jnp
import numpy as np
from jax import lax
from jax.sharding import PartitionSpec as P

D = 16384
LANES = 128
F32 = jnp.float32
BF16 = jnp.bfloat16


def sign_table(length):
    table = np.ones((1, 1), np.float32)
    while table.shape[0] < length:
        table = np.block([[table, table], [table, -table]])
    return table


def swap(value, mask):
    pairs = [(source, source ^ mask) for source in range(lax.axis_size("ch"))]
    return lax.ppermute(value, "ch", pairs)


def cross(values, my_index):
    for bit_pos in range(lax.axis_size("ch").bit_length() - 1):
        partner = swap(values, 2**bit_pos)
        upper = (my_index >> bit_pos & 1) == 1
        values = jnp.where(upper, partner - values, values + partner)
    return values


def local_transform(values, table, precision=None):
    rows, length = values.shape
    groups = [values[:, at : at + LANES] for at in range(0, length, LANES)]
    step = 1
    while step < len(groups):
        for low in range(len(groups)):
            if not low & step:
                first, second = groups[low], groups[low + step]
                groups[low], groups[low + step] = first + second, first - second
        step *= 2
    stacked = jnp.concatenate(groups, axis=0)
    done = jnp.dot(stacked, table.astype(values.dtype), precision=precision, preferred_element_type=F32)
    return jnp.concatenate([done[at : at + rows] for at in range(0, done.shape[0], rows)], axis=1)


def gather_tok(value):
    size = lax.axis_size("tok")
    copies = jnp.broadcast_to(value[None], (size,) + value.shape)
    return lax.all_to_all(copies, "tok", 0, 0, tiled=True)


def scatter_tok(value, send_type):
    size = lax.axis_size("tok")
    blocks = value.astype(send_type).reshape(size, value.shape[0] // size, value.shape[1])
    arrived = lax.all_to_all(blocks, "tok", 0, 0, tiled=True)
    return jnp.sum(arrived.astype(F32), axis=0)


def chip_groups():
    size = lax.axis_size("ch")
    return [[chip + core for chip in range(0, size, 2)] for core in range(2)]


def rows_of_core(value, core):
    size = lax.axis_size("ch")
    blocks = value.reshape(size // 2, 2, value.shape[0] // size, value.shape[1])
    chosen = lax.dynamic_index_in_dim(blocks, core, 1, keepdims=False)
    return chosen.reshape(value.shape[0] // 2, value.shape[1])


def scatter_ch(product, rows, core, swap_type, send_type):
    theirs = product(rows_of_core(rows, 1 - core)).astype(swap_type)
    arrived = swap(theirs, 1)
    mine = product(rows_of_core(rows, core))
    both = (mine + arrived.astype(F32)).astype(send_type)
    chips = lax.axis_size("ch") // 2
    blocks = both.reshape(chips, both.shape[0] // chips, both.shape[1])
    pieces = lax.all_to_all(blocks, "ch", 0, 0, tiled=True, axis_index_groups=chip_groups())
    return jnp.sum(pieces.astype(F32), axis=0)


def times(rows, weight):
    return jnp.dot(rows, weight, preferred_element_type=F32)


def times_t(rows, weight):
    return lax.dot_general(rows, weight, (((1,), (1,)), ((), ())), preferred_element_type=F32)


def on_device(tokens, probe, signs, gate_weight, up_weight, down_weight):
    tok_rows, channels = tokens.shape
    total_rows = tok_rows * lax.axis_size("tok")
    hidden = gate_weight.shape[1]
    my_index = lax.axis_index("ch")
    core = my_index & 1
    root_scale = 1.0 / math.sqrt(D)
    table = jnp.asarray(sign_table(LANES))
    probe_signs = (2 * probe - 1).astype(F32)
    channel_signs = (2 * signs - 1).astype(F32)

    all_tokens = gather_tok(tokens).reshape(total_rows, channels)
    token_part = jnp.stack([times(all_tokens, gate_weight), times(all_tokens, up_weight)], axis=1)
    token_sum = lax.psum_scatter(token_part, "ch", scatter_dimension=0, tiled=True)

    crossed = cross((probe_signs * channel_signs[None, :]).astype(BF16), my_index)
    tangent = (local_transform(crossed.astype(F32), table, lax.Precision.HIGHEST) * root_scale).astype(BF16)
    all_tangent = gather_tok(tangent).reshape(total_rows, channels)

    def gate_and_up(rows):
        return jnp.concatenate([times(rows, gate_weight), times(rows, up_weight)], axis=1)

    tangent_sum = scatter_ch(gate_and_up, all_tangent, core, BF16, BF16)

    gate_pre, up_pre = token_sum[:, 0], token_sum[:, 1]
    gate_tan, up_tan = tangent_sum[:, :hidden], tangent_sum[:, hidden:]
    sigmoid_gate = jax.nn.sigmoid(gate_pre)
    activated = gate_pre * sigmoid_gate
    slope_term = sigmoid_gate * (1.0 + gate_pre * (1.0 - sigmoid_gate))
    hidden_tan = (slope_term * gate_tan * up_pre + activated * up_tan).astype(BF16)

    out_part = times(lax.all_gather(hidden_tan, "ch", axis=0, tiled=True), down_weight)
    out_tangent = scatter_tok(out_part, F32).astype(BF16)
    all_out = gather_tok(out_tangent).reshape(total_rows, channels)

    back_hidden = scatter_ch(lambda rows: times_t(rows, down_weight), all_out, core, F32, BF16)
    back_gate = (back_hidden * up_pre * slope_term).astype(BF16)
    back_up = (back_hidden * activated).astype(BF16)
    back = jnp.concatenate([back_gate, back_up], axis=1)
    mine = lax.all_gather(back, "ch", axis=0, tiled=True, axis_index_groups=chip_groups())
    theirs = swap(mine, 1)

    def grad(rows):
        return times_t(rows[:, :hidden], gate_weight) + times_t(rows[:, hidden:], up_weight)

    in_mine, in_theirs = grad(mine), grad(theirs)
    split = (lax.axis_size("ch") // 2, tok_rows, channels)
    in_mine, in_theirs = in_mine.reshape(split), in_theirs.reshape(split)
    first = core == 0
    in_part = jnp.stack(
        [jnp.where(first, in_mine, in_theirs), jnp.where(first, in_theirs, in_mine)], axis=1
    ).reshape(total_rows, channels)
    back_tokens = scatter_tok(in_part, F32)

    local_back = local_transform(back_tokens, table, lax.Precision.HIGHEST)
    rotated_product = cross(local_back, my_index) * root_scale * channel_signs[None, :]
    token_terms = jnp.sum(probe_signs * rotated_product, axis=0)
    pieces = gather_tok(token_terms.reshape(-1, LANES))
    pieces = pieces.reshape(lax.axis_size("tok"), channels // LANES, LANES)
    diagonal_estimate = jnp.sum(pieces, axis=0).reshape(channels) / total_rows
    return (rotated_product, diagonal_estimate)


def solution(mesh):
    placed = (
        P("tok", "ch"),
        P("tok", "ch"),
        P("ch"),
        P("ch", "tok"),
        P("ch", "tok"),
        P("tok", "ch"),
    )
    return jax.shard_map(
        on_device, mesh=mesh, in_specs=placed, out_specs=(P("tok", "ch"), P("ch")), check_vma=False
    )
```

```python
import math

import jax
import jax.numpy as jnp
import numpy as np
from jax import lax
from jax.sharding import PartitionSpec as P

D = 16384
LANES = 128
F32 = jnp.float32
BF16 = jnp.bfloat16


def sign_table(length):
    table = np.ones((1, 1), np.float32)
    while table.shape[0] < length:
        table = np.block([[table, table], [table, -table]])
    return table


def swap(value, mask):
    pairs = [(source, source ^ mask) for source in range(lax.axis_size("ch"))]
    return lax.ppermute(value, "ch", pairs)


def cross(values, my_index, bits):
    for bit_pos in bits:
        partner = swap(values, 2**bit_pos)
        upper = (my_index >> bit_pos & 1) == 1
        values = jnp.where(upper, partner - values, values + partner)
    return values


def local_transform(values, table, precision=None):
    rows, length = values.shape
    groups = [values[:, at : at + LANES] for at in range(0, length, LANES)]
    step = 1
    while step < len(groups):
        for low in range(len(groups)):
            if not low & step:
                first, second = groups[low], groups[low + step]
                groups[low], groups[low + step] = first + second, first - second
        step *= 2
    stacked = jnp.concatenate(groups, axis=0)
    done = jnp.dot(stacked, table.astype(values.dtype), precision=precision, preferred_element_type=F32)
    return jnp.concatenate([done[at : at + rows] for at in range(0, done.shape[0], rows)], axis=1)


def gather_tok(value):
    size = lax.axis_size("tok")
    copies = jnp.broadcast_to(value[None], (size,) + value.shape)
    return lax.all_to_all(copies, "tok", 0, 0, tiled=True)


def scatter_tok(value, send_type):
    size = lax.axis_size("tok")
    blocks = value.astype(send_type).reshape(size, value.shape[0] // size, value.shape[1])
    arrived = lax.all_to_all(blocks, "tok", 0, 0, tiled=True)
    return jnp.sum(arrived.astype(F32), axis=0)


def chip_groups():
    size = lax.axis_size("ch")
    return [[chip + core for chip in range(0, size, 2)] for core in range(2)]


def rows_of_core(value, core):
    size = lax.axis_size("ch")
    blocks = value.reshape(size // 2, 2, value.shape[0] // size, value.shape[1])
    chosen = lax.dynamic_index_in_dim(blocks, core, 1, keepdims=False)
    return chosen.reshape(value.shape[0] // 2, value.shape[1])


def scatter_ch(product, rows, core, swap_type, send_type):
    theirs = product(rows_of_core(rows, 1 - core)).astype(swap_type)
    arrived = swap(theirs, 1)
    mine = product(rows_of_core(rows, core))
    both = (mine + arrived.astype(F32)).astype(send_type)
    chips = lax.axis_size("ch") // 2
    blocks = both.reshape(chips, both.shape[0] // chips, both.shape[1])
    pieces = lax.all_to_all(blocks, "ch", 0, 0, tiled=True, axis_index_groups=chip_groups())
    return jnp.sum(pieces.astype(F32), axis=0)


def gather_ch(value, core):
    chips = lax.axis_size("ch") // 2
    copies = jnp.broadcast_to(value[None], (chips,) + value.shape)
    mine = lax.all_to_all(copies, "ch", 0, 0, tiled=True, axis_index_groups=chip_groups())
    theirs = swap(mine, 1)
    first = core == 0
    return jnp.stack([jnp.where(first, mine, theirs), jnp.where(first, theirs, mine)], axis=1)


def times(rows, weight):
    return jnp.dot(rows, weight, preferred_element_type=F32)


def times_t(rows, weight):
    return lax.dot_general(rows, weight, (((1,), (1,)), ((), ())), preferred_element_type=F32)


def on_device(tokens, probe, signs, gate_weight, up_weight, down_weight):
    tok_rows, channels = tokens.shape
    total_rows = tok_rows * lax.axis_size("tok")
    hidden = gate_weight.shape[1]
    my_index = lax.axis_index("ch")
    core = my_index & 1
    root_scale = 1.0 / math.sqrt(D)
    table = jnp.asarray(sign_table(LANES))
    probe_signs = (2 * probe - 1).astype(F32)
    channel_signs = (2 * signs - 1).astype(F32)

    bits = list(range(lax.axis_size("ch").bit_length() - 1))
    all_tokens = gather_tok(tokens).reshape(total_rows, channels)
    crossed = cross((probe_signs * channel_signs[None, :]).astype(BF16), my_index, bits[:-1])
    crossed, all_tokens = lax.optimization_barrier((crossed, all_tokens))
    token_part = jnp.stack([times(all_tokens, gate_weight), times(all_tokens, up_weight)], axis=1)
    crossed = cross(crossed, my_index, bits[-1:])
    crossed, _ = lax.optimization_barrier((crossed, token_part))
    token_sum = lax.psum_scatter(token_part, "ch", scatter_dimension=0, tiled=True)
    tangent = (local_transform(crossed.astype(F32), table, lax.Precision.HIGHEST) * root_scale).astype(BF16)
    all_tangent = gather_tok(tangent).reshape(total_rows, channels)

    def gate_and_up(rows):
        return jnp.concatenate([times(rows, gate_weight), times(rows, up_weight)], axis=1)

    tangent_sum = scatter_ch(gate_and_up, all_tangent, core, BF16, BF16)

    gate_pre, up_pre = token_sum[:, 0], token_sum[:, 1]
    gate_tan, up_tan = tangent_sum[:, :hidden], tangent_sum[:, hidden:]
    sigmoid_gate = jax.nn.sigmoid(gate_pre)
    activated = gate_pre * sigmoid_gate
    slope_term = sigmoid_gate * (1.0 + gate_pre * (1.0 - sigmoid_gate))
    hidden_tan = (slope_term * gate_tan * up_pre + activated * up_tan).astype(BF16)

    out_part = times(lax.all_gather(hidden_tan, "ch", axis=0, tiled=True), down_weight)
    out_tangent = scatter_tok(out_part, BF16).astype(BF16)
    all_out = gather_tok(out_tangent).reshape(total_rows, channels)

    back_hidden = scatter_ch(lambda rows: times_t(rows, down_weight), all_out, core, F32, BF16)
    back_gate = (back_hidden * up_pre * slope_term).astype(BF16)
    back_up = (back_hidden * activated).astype(BF16)
    back = jnp.concatenate([back_gate, back_up], axis=1)
    all_back = gather_ch(back, core).reshape(total_rows, 2 * hidden)
    in_part = times_t(all_back[:, :hidden], gate_weight) + times_t(all_back[:, hidden:], up_weight)
    back_tokens = scatter_tok(in_part, BF16)

    local_back = local_transform(back_tokens, table, lax.Precision.HIGHEST)
    rotated_product = cross(local_back, my_index, bits) * root_scale * channel_signs[None, :]
    token_terms = jnp.sum(probe_signs * rotated_product, axis=0)
    pieces = gather_tok(token_terms.reshape(-1, LANES))
    pieces = pieces.reshape(lax.axis_size("tok"), channels // LANES, LANES)
    diagonal_estimate = jnp.sum(pieces, axis=0).reshape(channels) / total_rows
    return (rotated_product, diagonal_estimate)


def solution(mesh):
    placed = (
        P("tok", "ch"),
        P("tok", "ch"),
        P("ch"),
        P("ch", "tok"),
        P("ch", "tok"),
        P("tok", "ch"),
    )
    return jax.shard_map(
        on_device, mesh=mesh, in_specs=placed, out_specs=(P("tok", "ch"), P("ch")), check_vma=False
    )
```

```python
import math

import jax
import jax.numpy as jnp
import numpy as np
from jax import lax
from jax.sharding import PartitionSpec as P

D = 16384
LANES = 128
F32 = jnp.float32
BF16 = jnp.bfloat16
F16 = jnp.float16


def sign_table(length):
    table = np.ones((1, 1), np.float32)
    while table.shape[0] < length:
        table = np.block([[table, table], [table, -table]])
    return table


def swap(value, mask):
    pairs = [(source, source ^ mask) for source in range(lax.axis_size("ch"))]
    return lax.ppermute(value, "ch", pairs)


def bit_sign(my_index, bit_pos, dtype):
    return (1 - 2 * (my_index >> bit_pos & 1)).astype(dtype)


def cross(values, my_index, bits):
    for bit_pos in bits:
        values = swap(values, 2**bit_pos) + values * bit_sign(my_index, bit_pos, values.dtype)
    return values


def cross_two(values, my_index, low, high):
    low_sign = bit_sign(my_index, low, values.dtype)
    high_sign = bit_sign(my_index, high, values.dtype)
    both = swap(values, 2**low + 2**high)
    from_high = swap(values, 2**high)
    from_low = swap(values, 2**low)
    return (both + from_high * low_sign) + (from_low * high_sign + values * (low_sign * high_sign))


def local_transform(values, table, precision=None):
    rows, length = values.shape
    groups = [values[:, at : at + LANES] for at in range(0, length, LANES)]
    step = 1
    while step < len(groups):
        for low in range(len(groups)):
            if not low & step:
                first, second = groups[low], groups[low + step]
                groups[low], groups[low + step] = first + second, first - second
        step *= 2
    stacked = jnp.concatenate(groups, axis=0)
    done = jnp.dot(stacked, table.astype(values.dtype), precision=precision, preferred_element_type=F32)
    return jnp.concatenate([done[at : at + rows] for at in range(0, done.shape[0], rows)], axis=1)


def gather_tok(value):
    size = lax.axis_size("tok")
    copies = jnp.broadcast_to(value[None], (size,) + value.shape)
    return lax.all_to_all(copies, "tok", 0, 0, tiled=True)


def scatter_tok(value, send_type):
    size = lax.axis_size("tok")
    blocks = value.astype(send_type).reshape(size, value.shape[0] // size, value.shape[1])
    arrived = lax.all_to_all(blocks, "tok", 0, 0, tiled=True)
    return jnp.sum(arrived.astype(F32), axis=0)


def chip_groups():
    size = lax.axis_size("ch")
    return [[chip + core for chip in range(0, size, 2)] for core in range(2)]


def rows_of_core(value, core):
    size = lax.axis_size("ch")
    blocks = value.reshape(size // 2, 2, value.shape[0] // size, value.shape[1])
    chosen = lax.dynamic_index_in_dim(blocks, core, 1, keepdims=False)
    return chosen.reshape(value.shape[0] // 2, value.shape[1])


def sum_on_chip(products, rows, core):
    their_rows, my_rows = rows_of_core(rows, 1 - core), rows_of_core(rows, core)
    arrived = [swap(product(their_rows), 1) for product in products]
    return [product(my_rows) + other for product, other in zip(products, arrived)]


def to_chips(value):
    chips = lax.axis_size("ch") // 2
    blocks = value.reshape(chips, value.shape[0] // chips, value.shape[1])
    return lax.all_to_all(blocks, "ch", 0, 0, tiled=True, axis_index_groups=chip_groups())


def pack(parts):
    lane = lax.broadcasted_iota(jnp.int32, (parts[0].shape[0], LANES), 1)
    scaled, exponents = [], jnp.zeros(lane.shape, F32)
    for at, part in enumerate(parts):
        peak = jnp.max(jnp.abs(part), axis=1, keepdims=True)
        exponent = jnp.clip(jnp.round(jnp.log2(peak)), -120.0, 120.0)
        scaled.append((part * jnp.exp2(-exponent)).astype(F16))
        exponents = jnp.where(lane == at, exponent, exponents)
    return jnp.concatenate(scaled + [exponents.astype(F16)], axis=1)


def unpack_sum(pieces, count):
    width = (pieces.shape[2] - LANES) // count
    tail = lax.optimization_barrier(pieces[:, :, count * width :]).astype(F32)
    lane = lax.broadcasted_iota(jnp.int32, tail.shape, 2)
    sums = []
    for at in range(count):
        exponent = jnp.sum(jnp.where(lane == at, tail, 0.0), axis=2, keepdims=True)
        part = pieces[:, :, at * width : (at + 1) * width].astype(F32)
        sums.append(jnp.sum(part * jnp.exp2(exponent), axis=0))
    return sums


def times(rows, weight):
    return jnp.dot(rows, weight, preferred_element_type=F32)


def times_t(rows, weight):
    return lax.dot_general(rows, weight, (((1,), (1,)), ((), ())), preferred_element_type=F32)


def on_device(tokens, probe, signs, gate_weight, up_weight, down_weight):
    tok_rows, channels = tokens.shape
    total_rows = tok_rows * lax.axis_size("tok")
    hidden = gate_weight.shape[1]
    my_index = lax.axis_index("ch")
    core = my_index & 1
    root_scale = 1.0 / math.sqrt(D)
    table = jnp.asarray(sign_table(LANES))
    probe_signs = (2 * probe - 1).astype(F32)
    channel_signs = (2 * signs - 1).astype(F32)

    all_tokens = gather_tok(tokens).reshape(total_rows, channels)
    crossed = cross((probe_signs * channel_signs[None, :]).astype(BF16), my_index, (0, 1, 2))
    crossed, all_tokens = lax.optimization_barrier((crossed, all_tokens))
    token_part = jnp.stack([times(all_tokens, gate_weight), times(all_tokens, up_weight)], axis=1)
    crossed = cross(crossed, my_index, (3,))
    crossed, _ = lax.optimization_barrier((crossed, token_part))
    token_sum = lax.psum_scatter(token_part, "ch", scatter_dimension=0, tiled=True)
    tangent = (local_transform(crossed.astype(F32), table, lax.Precision.HIGHEST) * root_scale).astype(BF16)
    all_tangent = gather_tok(tangent).reshape(total_rows, channels)
    gate_and_up = [lambda rows: times(rows, gate_weight), lambda rows: times(rows, up_weight)]
    tangent_pieces = to_chips(pack(sum_on_chip(gate_and_up, all_tangent, core)))

    gate_pre, up_pre = token_sum[:, 0], token_sum[:, 1]
    gate_tan, up_tan = unpack_sum(tangent_pieces, 2)
    sigmoid_gate = jax.nn.sigmoid(gate_pre)
    activated = gate_pre * sigmoid_gate
    slope_term = sigmoid_gate * (1.0 + gate_pre * (1.0 - sigmoid_gate))
    hidden_tan = (slope_term * gate_tan * up_pre + activated * up_tan).astype(BF16)

    factors = jnp.concatenate([(up_pre * slope_term).astype(BF16), activated.astype(BF16)], axis=1)
    all_factors = lax.all_gather(factors, "ch", axis=0, tiled=True)

    out_part = times(lax.all_gather(hidden_tan, "ch", axis=0, tiled=True), down_weight)
    out_tangent = scatter_tok(out_part, BF16).astype(BF16)
    all_out = gather_tok(out_tangent).reshape(total_rows, channels)

    back_part = sum_on_chip([lambda rows: times_t(rows, down_weight)], all_out, core)[0]
    back_hidden = jnp.sum(to_chips(back_part.astype(BF16)).astype(F32), axis=0)
    all_back = lax.all_gather(back_hidden.astype(BF16), "ch", axis=0, tiled=True).astype(F32)
    back_gate = (all_back * all_factors[:, :hidden].astype(F32)).astype(BF16)
    back_up = (all_back * all_factors[:, hidden:].astype(F32)).astype(BF16)
    in_part = times_t(back_gate, gate_weight) + times_t(back_up, up_weight)
    back_tokens = scatter_tok(in_part, BF16)

    local_back = local_transform(back_tokens, table, lax.Precision.HIGHEST)
    local_back = cross_two(cross(local_back, my_index, (0, 1)), my_index, 2, 3)
    rotated_product = local_back * root_scale * channel_signs[None, :]
    token_terms = jnp.sum(probe_signs * rotated_product, axis=0)
    pieces = gather_tok(token_terms.reshape(-1, LANES))
    pieces = pieces.reshape(lax.axis_size("tok"), channels // LANES, LANES)
    diagonal_estimate = jnp.sum(pieces, axis=0).reshape(channels) / total_rows
    return (rotated_product, diagonal_estimate)


def solution(mesh):
    placed = (
        P("tok", "ch"),
        P("tok", "ch"),
        P("ch"),
        P("ch", "tok"),
        P("ch", "tok"),
        P("tok", "ch"),
    )
    return jax.shard_map(
        on_device, mesh=mesh, in_specs=placed, out_specs=(P("tok", "ch"), P("ch")), check_vma=False
    )
```

```python
import math

import jax
import jax.numpy as jnp
import numpy as np
from jax import lax
from jax.sharding import PartitionSpec as P

D = 16384
LANES = 128
F32 = jnp.float32
BF16 = jnp.bfloat16
F16 = jnp.float16


def sign_table(length):
    table = np.ones((1, 1), np.float32)
    while table.shape[0] < length:
        table = np.block([[table, table], [table, -table]])
    return table


def swap(value, mask):
    pairs = [(source, source ^ mask) for source in range(lax.axis_size("ch"))]
    return lax.ppermute(value, "ch", pairs)


def bit_sign(my_index, bit_pos, dtype):
    return (1 - 2 * (my_index >> bit_pos & 1)).astype(dtype)


def cross(values, my_index, bits):
    for bit_pos in bits:
        values = swap(values, 2**bit_pos) + values * bit_sign(my_index, bit_pos, values.dtype)
    return values


def cross_two(values, my_index, low, high):
    low_sign = bit_sign(my_index, low, values.dtype)
    high_sign = bit_sign(my_index, high, values.dtype)
    both = swap(values, 2**low + 2**high)
    from_high = swap(values, 2**high)
    from_low = swap(values, 2**low)
    return (both + from_high * low_sign) + (from_low * high_sign + values * (low_sign * high_sign))


def local_transform(values, table, precision=None):
    rows, length = values.shape
    groups = [values[:, at : at + LANES] for at in range(0, length, LANES)]
    step = 1
    while step < len(groups):
        for low in range(len(groups)):
            if not low & step:
                first, second = groups[low], groups[low + step]
                groups[low], groups[low + step] = first + second, first - second
        step *= 2
    stacked = jnp.concatenate(groups, axis=0)
    done = jnp.dot(stacked, table.astype(values.dtype), precision=precision, preferred_element_type=F32)
    return jnp.concatenate([done[at : at + rows] for at in range(0, done.shape[0], rows)], axis=1)


def gather_tok(value):
    size = lax.axis_size("tok")
    copies = jnp.broadcast_to(value[None], (size,) + value.shape)
    return lax.all_to_all(copies, "tok", 0, 0, tiled=True)


def scatter_tok(value, send_type):
    size = lax.axis_size("tok")
    blocks = value.astype(send_type).reshape(size, value.shape[0] // size, value.shape[1])
    arrived = lax.all_to_all(blocks, "tok", 0, 0, tiled=True)
    return jnp.sum(arrived.astype(F32), axis=0)


def chip_groups():
    size = lax.axis_size("ch")
    return [[chip + core for chip in range(0, size, 2)] for core in range(2)]


def rows_of_core(value, core):
    size = lax.axis_size("ch")
    blocks = value.reshape(size // 2, 2, value.shape[0] // size, value.shape[1])
    chosen = lax.dynamic_index_in_dim(blocks, core, 1, keepdims=False)
    return chosen.reshape(value.shape[0] // 2, value.shape[1])


def sum_on_chip(products, rows, core):
    their_rows, my_rows = rows_of_core(rows, 1 - core), rows_of_core(rows, core)
    arrived = [swap(product(their_rows), 1) for product in products]
    return [product(my_rows) + other for product, other in zip(products, arrived)]


def to_chips(value):
    chips = lax.axis_size("ch") // 2
    blocks = value.reshape(chips, value.shape[0] // chips, value.shape[1])
    return lax.all_to_all(blocks, "ch", 0, 0, tiled=True, axis_index_groups=chip_groups())


def pack(parts):
    lane = lax.broadcasted_iota(jnp.int32, (parts[0].shape[0], LANES), 1)
    scaled, exponents = [], jnp.zeros(lane.shape, F32)
    for at, part in enumerate(parts):
        peak = jnp.max(jnp.abs(part), axis=1, keepdims=True)
        exponent = jnp.clip(jnp.round(jnp.log2(peak)), -120.0, 120.0)
        scaled.append((part * jnp.exp2(-exponent)).astype(F16))
        exponents = jnp.where(lane == at, exponent, exponents)
    return jnp.concatenate(scaled + [exponents.astype(F16)], axis=1)


def unpack_sum(pieces, count):
    width = (pieces.shape[2] - LANES) // count
    tail = lax.optimization_barrier(pieces[:, :, count * width :]).astype(F32)
    lane = lax.broadcasted_iota(jnp.int32, tail.shape, 2)
    sums = []
    for at in range(count):
        exponent = jnp.sum(jnp.where(lane == at, tail, 0.0), axis=2, keepdims=True)
        part = pieces[:, :, at * width : (at + 1) * width].astype(F32)
        sums.append(jnp.sum(part * jnp.exp2(exponent), axis=0))
    return sums


def times(rows, weight):
    return jnp.dot(rows, weight, preferred_element_type=F32)


def times_t(rows, weight):
    return lax.dot_general(rows, weight, (((1,), (1,)), ((), ())), preferred_element_type=F32)


def on_device(tokens, probe, signs, gate_weight, up_weight, down_weight):
    tok_rows, channels = tokens.shape
    total_rows = tok_rows * lax.axis_size("tok")
    hidden = gate_weight.shape[1]
    my_index = lax.axis_index("ch")
    core = my_index & 1
    root_scale = 1.0 / math.sqrt(D)
    table = jnp.asarray(sign_table(LANES))
    probe_signs = (2 * probe - 1).astype(F32)
    channel_signs = (2 * signs - 1).astype(F32)

    all_tokens = gather_tok(tokens).reshape(total_rows, channels)
    crossed = cross_two(jnp.where(probe == signs[None, :], 1.0, -1.0).astype(BF16), my_index, 0, 1)
    crossed = cross(crossed, my_index, (2,))
    crossed, all_tokens = lax.optimization_barrier((crossed, all_tokens))
    token_part = jnp.stack([times(all_tokens, gate_weight), times(all_tokens, up_weight)], axis=1)
    crossed = cross(crossed, my_index, (3,))
    crossed, _ = lax.optimization_barrier((crossed, token_part))
    token_sum = lax.psum_scatter(token_part, "ch", scatter_dimension=0, tiled=True)
    tangent = (local_transform(crossed.astype(F32), table, lax.Precision.HIGHEST) * root_scale).astype(BF16)
    all_tangent = gather_tok(tangent).reshape(total_rows, channels)
    gate_and_up = [lambda rows: times(rows, gate_weight), lambda rows: times(rows, up_weight)]
    tangent_pieces = to_chips(pack(sum_on_chip(gate_and_up, all_tangent, core)))

    gate_pre, up_pre = token_sum[:, 0], token_sum[:, 1]
    gate_tan, up_tan = unpack_sum(tangent_pieces, 2)
    sigmoid_gate = jax.nn.sigmoid(gate_pre)
    activated = gate_pre * sigmoid_gate
    slope_term = sigmoid_gate * (1.0 + gate_pre * (1.0 - sigmoid_gate))
    hidden_tan = (slope_term * gate_tan * up_pre + activated * up_tan).astype(BF16)

    factors = jnp.concatenate([(up_pre * slope_term).astype(BF16), activated.astype(BF16)], axis=1)
    all_factors = lax.all_gather(factors, "ch", axis=0, tiled=True)

    out_part = times(lax.all_gather(hidden_tan, "ch", axis=0, tiled=True), down_weight)
    out_tangent = scatter_tok(out_part, BF16).astype(BF16)
    all_out = gather_tok(out_tangent).reshape(total_rows, channels)

    back_part = times_t(all_out, down_weight)
    back_part = rows_of_core(back_part, core) + swap(rows_of_core(back_part, 1 - core), 1)
    back_hidden = jnp.sum(to_chips(back_part.astype(BF16)).astype(F32), axis=0)
    all_back = lax.all_gather(back_hidden.astype(BF16), "ch", axis=0, tiled=True).astype(F32)
    back_gate = (all_back * all_factors[:, :hidden].astype(F32)).astype(BF16)
    back_up = (all_back * all_factors[:, hidden:].astype(F32)).astype(BF16)
    in_part = times_t(back_gate, gate_weight) + times_t(back_up, up_weight)
    back_tokens = scatter_tok(in_part, BF16)

    local_back = local_transform(back_tokens, table, lax.Precision.HIGHEST)
    local_back = cross_two(cross_two(local_back, my_index, 0, 1), my_index, 2, 3)
    rotated_product = local_back * root_scale * channel_signs[None, :]
    token_terms = jnp.sum(probe_signs * rotated_product, axis=0)
    pieces = gather_tok(token_terms.reshape(-1, LANES))
    pieces = pieces.reshape(lax.axis_size("tok"), channels // LANES, LANES)
    diagonal_estimate = jnp.sum(pieces, axis=0).reshape(channels) / total_rows
    return (rotated_product, diagonal_estimate)


def solution(mesh):
    placed = (
        P("tok", "ch"),
        P("tok", "ch"),
        P("ch"),
        P("ch", "tok"),
        P("ch", "tok"),
        P("tok", "ch"),
    )
    return jax.shard_map(
        on_device, mesh=mesh, in_specs=placed, out_specs=(P("tok", "ch"), P("ch")), check_vma=False
    )
```

```python
import math

import jax
import jax.numpy as jnp
import numpy as np
from jax import lax
from jax.sharding import PartitionSpec as P

D = 16384
LANES = 128
F32 = jnp.float32
BF16 = jnp.bfloat16
F16 = jnp.float16


def sign_table(length):
    table = np.ones((1, 1), np.float32)
    while table.shape[0] < length:
        table = np.block([[table, table], [table, -table]])
    return table


def swap(value, mask):
    pairs = [(source, source ^ mask) for source in range(lax.axis_size("ch"))]
    return lax.ppermute(value, "ch", pairs)


def bit_sign(my_index, bit_pos, dtype):
    return (1 - 2 * (my_index >> bit_pos & 1)).astype(dtype)


def cross(values, my_index, bits):
    for bit_pos in bits:
        values = swap(values, 2**bit_pos) + values * bit_sign(my_index, bit_pos, values.dtype)
    return values


def cross_two(values, my_index, low, high):
    low_sign = bit_sign(my_index, low, values.dtype)
    high_sign = bit_sign(my_index, high, values.dtype)
    from_low = swap(values, 2**low)
    both = swap(values, 2**low + 2**high)
    from_high = swap(values, 2**high)
    far = from_high * low_sign + values * (low_sign * high_sign)
    return far + (from_low * high_sign + both)


def local_transform(values, table, precision=None):
    rows, length = values.shape
    groups = [values[:, at : at + LANES] for at in range(0, length, LANES)]
    step = 1
    while step < len(groups):
        for low in range(len(groups)):
            if not low & step:
                first, second = groups[low], groups[low + step]
                groups[low], groups[low + step] = first + second, first - second
        step *= 2
    stacked = jnp.concatenate(groups, axis=0)
    done = jnp.dot(stacked, table.astype(values.dtype), precision=precision, preferred_element_type=F32)
    return jnp.concatenate([done[at : at + rows] for at in range(0, done.shape[0], rows)], axis=1)


def gather_tok(value):
    size = lax.axis_size("tok")
    copies = jnp.broadcast_to(value[None], (size,) + value.shape)
    return lax.all_to_all(copies, "tok", 0, 0, tiled=True)


def scatter_tok(value, send_type):
    size = lax.axis_size("tok")
    blocks = value.astype(send_type).reshape(size, value.shape[0] // size, value.shape[1])
    arrived = lax.all_to_all(blocks, "tok", 0, 0, tiled=True)
    return jnp.sum(arrived.astype(F32), axis=0)


def chip_groups():
    size = lax.axis_size("ch")
    return [[chip + core for chip in range(0, size, 2)] for core in range(2)]


def rows_of_core(value, core):
    size = lax.axis_size("ch")
    blocks = value.reshape(size // 2, 2, value.shape[0] // size, value.shape[1])
    chosen = lax.dynamic_index_in_dim(blocks, core, 1, keepdims=False)
    return chosen.reshape(value.shape[0] // 2, value.shape[1])


def sum_on_chip(products, rows, core):
    their_rows, my_rows = rows_of_core(rows, 1 - core), rows_of_core(rows, core)
    arrived = [swap(product(their_rows), 1) for product in products]
    return [product(my_rows) + other for product, other in zip(products, arrived)]


def to_chips(value):
    chips = lax.axis_size("ch") // 2
    blocks = value.reshape(chips, value.shape[0] // chips, value.shape[1])
    return lax.all_to_all(blocks, "ch", 0, 0, tiled=True, axis_index_groups=chip_groups())


def pack(parts):
    lane = lax.broadcasted_iota(jnp.int32, (parts[0].shape[0], LANES), 1)
    scaled, exponents = [], jnp.zeros(lane.shape, F32)
    for at, part in enumerate(parts):
        peak = jnp.max(jnp.abs(part), axis=1, keepdims=True)
        exponent = jnp.clip(jnp.round(jnp.log2(peak)), -120.0, 120.0)
        scaled.append((part * jnp.exp2(-exponent)).astype(F16))
        exponents = jnp.where(lane == at, exponent, exponents)
    return jnp.concatenate(scaled + [exponents.astype(F16)], axis=1)


def unpack_sum(pieces, count):
    width = (pieces.shape[2] - LANES) // count
    tail = lax.optimization_barrier(pieces[:, :, count * width :]).astype(F32)
    lane = lax.broadcasted_iota(jnp.int32, tail.shape, 2)
    sums = []
    for at in range(count):
        exponent = jnp.sum(jnp.where(lane == at, tail, 0.0), axis=2, keepdims=True)
        part = pieces[:, :, at * width : (at + 1) * width].astype(F32)
        sums.append(jnp.sum(part * jnp.exp2(exponent), axis=0))
    return sums


def times(rows, weight):
    return jnp.dot(rows, weight, preferred_element_type=F32)


def times_t(rows, weight):
    return lax.dot_general(rows, weight, (((1,), (1,)), ((), ())), preferred_element_type=F32)


def on_device(tokens, probe, signs, gate_weight, up_weight, down_weight):
    tok_rows, channels = tokens.shape
    total_rows = tok_rows * lax.axis_size("tok")
    hidden = gate_weight.shape[1]
    my_index = lax.axis_index("ch")
    core = my_index & 1
    root_scale = 1.0 / math.sqrt(D)
    table = jnp.asarray(sign_table(LANES))
    probe_signs = (2 * probe - 1).astype(F32)
    channel_signs = (2 * signs - 1).astype(F32)

    all_tokens = gather_tok(tokens).reshape(total_rows, channels)
    crossed = cross_two(jnp.where(probe == signs[None, :], 1.0, -1.0).astype(BF16), my_index, 0, 1)
    crossed = cross(crossed, my_index, (2,))
    crossed, all_tokens = lax.optimization_barrier((crossed, all_tokens))
    token_part = jnp.stack([times(all_tokens, gate_weight), times(all_tokens, up_weight)], axis=1)
    crossed = cross(crossed, my_index, (3,))
    crossed, _ = lax.optimization_barrier((crossed, token_part))
    token_sum = lax.psum_scatter(token_part, "ch", scatter_dimension=0, tiled=True)
    tangent = (local_transform(crossed.astype(F32), table, lax.Precision.HIGHEST) * root_scale).astype(BF16)
    all_tangent = gather_tok(tangent).reshape(total_rows, channels)
    gate_and_up = [lambda rows: times(rows, gate_weight), lambda rows: times(rows, up_weight)]
    tangent_pieces = to_chips(pack(sum_on_chip(gate_and_up, all_tangent, core)))

    gate_pre, up_pre = token_sum[:, 0], token_sum[:, 1]
    gate_tan, up_tan = unpack_sum(tangent_pieces, 2)
    sigmoid_gate = jax.nn.sigmoid(gate_pre)
    activated = gate_pre * sigmoid_gate
    slope_term = sigmoid_gate * (1.0 + gate_pre * (1.0 - sigmoid_gate))
    hidden_tan = (slope_term * gate_tan * up_pre + activated * up_tan).astype(BF16)

    factors = jnp.concatenate([(up_pre * slope_term).astype(BF16), activated.astype(BF16)], axis=1)
    all_factors = lax.all_gather(factors, "ch", axis=0, tiled=True)

    out_part = times(lax.all_gather(hidden_tan, "ch", axis=0, tiled=True), down_weight)
    out_tangent = scatter_tok(out_part, BF16).astype(BF16)
    all_out = gather_tok(out_tangent).reshape(total_rows, channels)

    back_part = times_t(all_out, down_weight)
    back_part = rows_of_core(back_part, core) + swap(rows_of_core(back_part, 1 - core), 1)
    back_hidden = jnp.sum(to_chips(back_part.astype(BF16)).astype(F32), axis=0)
    all_back = lax.all_gather(back_hidden.astype(BF16), "ch", axis=0, tiled=True).astype(F32)
    back_gate = (all_back * all_factors[:, :hidden].astype(F32)).astype(BF16)
    back_up = (all_back * all_factors[:, hidden:].astype(F32)).astype(BF16)
    in_part = times_t(back_gate, gate_weight) + times_t(back_up, up_weight)
    back_tokens = scatter_tok(in_part, BF16)

    local_back = local_transform(back_tokens, table, lax.Precision.HIGHEST)
    local_back = cross_two(cross_two(local_back, my_index, 0, 1), my_index, 2, 3)
    rotated_product = local_back * root_scale * channel_signs[None, :]
    token_terms = jnp.sum(probe_signs * rotated_product, axis=0)
    pieces = gather_tok(token_terms.reshape(-1, LANES))
    pieces = pieces.reshape(lax.axis_size("tok"), channels // LANES, LANES)
    diagonal_estimate = jnp.sum(pieces, axis=0).reshape(channels) / total_rows
    return (rotated_product, diagonal_estimate)


def solution(mesh):
    placed = (
        P("tok", "ch"),
        P("tok", "ch"),
        P("ch"),
        P("ch", "tok"),
        P("ch", "tok"),
        P("tok", "ch"),
    )
    return jax.shard_map(
        on_device, mesh=mesh, in_specs=placed, out_specs=(P("tok", "ch"), P("ch")), check_vma=False
    )
```
